32 devices in a mesh: groups: 2 (over x), tm: 16 (over z, y, core).
Axes of the slice: x: 2, y: 2, z: 4, core: 2. Of those that a mesh axis runs over, the one named last changes fastest.
Arguments:
- state: float32 [32, 64, 1, 1440], P(('groups', 'tm')), parts along dimension 0, may hold values from -18 to 18
- observed: float32 [32, 64, 1, 1440], P(('groups', 'tm')), parts along dimension 0, may hold values from -6 to 6
- obs_mask: int32 [32, 64, 1, 1440], P(('groups', 'tm')), parts along dimension 0, may hold values 0 or 1
- noise: float32 [32, 64, 1, 1440], P(('groups', 'tm')), parts along dimension 0, may hold values from -6 to 6
- w_first: bfloat16 [256, 320, 3, 3], replicated, may hold values from -0.109375 to 0.109375
- b_first: float32 [256], replicated, may hold values from -3 to 3
- w_second: bfloat16 [64, 256, 3, 3], replicated, may hold values from -0.125 to 0.125
- b_second: float32 [64], replicated, may hold values from -3 to 3
Outputs:
- sample: float32 [32, 64, 1, 1440], P(('groups', 'tm')), parts along dimension 0
The draws below stay inside these ranges and needn't reach their ends.
There are 2 independent parts, one for each index of `groups`. The reference program is written for one: setup_inputs(seed, part) draws one part's arguments, and reference() takes and returns one part's arrays. A program takes and returns all parts, laid end to end along the dimension named above; an argument that names none is the same for every part. Nothing has to cross between parts.
All inputs are finite; a program needn't handle non-finite values. No bound on the sum of `obs_mask` on one device may be relied on, other than what follows from the above.
Results may differ from the reference program's by a relative error of at most 0.00048.
Values may be sent and summed in bfloat16 or wider, within the bound.
No kernel may reach another device: no remote copies, remote signals or barrier semaphores. Data moves between devices by JAX's collectives and lax.ppermute only.
A program may use at most 64 MiB of HBM per device.

```python
import jax
import jax.numpy as jnp
from jax import lax

VARS = 64
HID = 256
WIN = 5
LAT = 1
LON = 1440
HOURS = 16


def draw_state(key, part):
    key_a = jax.random.fold_in(key, 11)
    key_b = jax.random.fold_in(key, 12)
    hour_scale = 1.0 + 2.0 * jnp.arange(HOURS, dtype=jnp.float32) / max(HOURS - 1, 1)
    var_scale = jnp.exp(jax.random.uniform(key_b, (1, VARS, LAT, 1), jnp.float32, -0.69, 0.69))
    shape = (HOURS, VARS, LAT, LON)
    base = jnp.clip(jax.random.normal(key_a, shape, jnp.float32), -3.0, 3.0)
    return hour_scale[:, None, None, None] * var_scale * base


def set_ends(drawn, rng, least, high):
    extent = drawn.shape
    place = [jax.random.randint(jax.random.fold_in(rng, axis), (), 0, extent[axis]) for axis in range(len(extent))]
    drawn = drawn.at[tuple(place)].set(least)
    longest = extent.index(max(extent))
    place[longest] = (place[longest] + 1) % extent[longest]
    return drawn.at[tuple(place)].set(high)


def block_scale(own_key, extent, pieces, least, largest):
    def one(dim, blocks):
        draws = jax.random.uniform(jax.random.fold_in(jax.random.fold_in(own_key, 6), dim), (blocks,), jnp.float32, least / len(pieces), largest / len(pieces))
        return jnp.repeat(jnp.exp(draws), extent[dim] // blocks).reshape((-1,) + (1,) * (len(extent) - dim - 1))

    factor_of = one(*pieces[0])
    for cut in pieces[1:]:
        factor_of = factor_of * one(*cut)
    return factor_of


def centred(own_key, dims, scale, reach, split=(), kind=jnp.bfloat16):
    gain = block_scale(own_key, dims, split, -0.22, 0.18) if split else 1.0
    array = jax.random.normal(own_key, dims, jnp.float32) * scale * gain
    return jnp.minimum(jnp.maximum(array, -reach), reach).astype(kind)


def setup_inputs(seed: int = 0, part: int = 0) -> dict:
    key_list = jax.random.split(jax.random.key(seed), 9)
    part_splits = jax.random.split(jax.random.fold_in(key_list[8], part), 9)
    state = draw_state(jax.random.fold_in(jax.random.fold_in(key_list[8], part), 71), part)
    observed = centred(part_splits[1], (HOURS, VARS, LAT, LON), 1.0, 6.0, ((0, 16),), jnp.float32)
    obs_mask = set_ends((jax.random.randint(part_splits[2], (HOURS, VARS, LAT, LON), 0, 4) < 1).astype(jnp.int32), jax.random.fold_in(part_splits[2], 1), 0, 1)
    noise = centred(part_splits[3], (HOURS, VARS, LAT, LON), 1.0, 6.0, ((0, 16),), jnp.float32)
    w_first = centred(key_list[4], (HID, WIN * VARS, 3, 3), (9 * WIN * VARS) ** -0.5, 0.109375)
    b_first = centred(key_list[5], (HID,), 0.5, 3.0, (), jnp.float32)
    w_second = centred(key_list[6], (VARS, HID, 3, 3), (9 * HID) ** -0.5, 0.125)
    b_second = centred(key_list[7], (VARS,), 0.5, 3.0, (), jnp.float32)
    return {"state": state, "observed": observed, "obs_mask": obs_mask, "noise": noise, "w_first": w_first, "b_first": b_first, "w_second": w_second, "b_second": b_second}


def conv_wrap(field, weights):
    wrapped = jnp.concatenate([field[..., -1:], field, field[..., :1]], axis=-1)
    padded = jnp.pad(wrapped, ((0, 0), (0, 0), (1, 1), (0, 0)))
    return lax.conv_general_dilated(padded, weights, (1, 1), 'VALID', dimension_numbers=('NCHW', 'OIHW', 'NCHW'), preferred_element_type=jnp.float32)

def score(field, observed, mask_f, w_first, b_first, w_second, b_second):
    rounded = field.astype(jnp.bfloat16)
    padded = jnp.pad(rounded, ((2, 2), (0, 0), (0, 0), (0, 0)))
    window = jnp.concatenate([padded[k:k + HOURS] for k in range(WIN)], axis=1)
    pre = conv_wrap(window, w_first) + b_first[None, :, None, None]
    hidden = jax.nn.silu(pre).astype(jnp.bfloat16)
    out = conv_wrap(hidden, w_second) + b_second[None, :, None, None]
    return out + mask_f * (observed - field)

def reference(state, observed, obs_mask, noise, w_first, b_first, w_second, b_second):
    mask_f = obs_mask.astype(jnp.float32)
    predicted = state + 0.5 * score(state, observed, mask_f, w_first, b_first, w_second, b_second)
    drift = score(predicted, observed, mask_f, w_first, b_first, w_second, b_second)
    zsq = jnp.sum(noise * noise)
    gsq = jnp.sum(drift * drift)
    step = 2.0 * 0.16 * 0.16 * zsq / (gsq + 1e-06)
    return predicted + step * drift + jnp.sqrt(2.0 * step) * noise
```

```python
import functools

import jax
import jax.numpy as jnp
from jax import lax
from jax.experimental import pallas as pl
from jax.experimental.pallas import tpu as pltpu
from jax.sharding import PartitionSpec as P

LANES = 128
TILE = 256
VMEM = pl.BlockSpec(memory_space=pltpu.VMEM)
SMEM = pl.BlockSpec(memory_space=pltpu.SMEM)


def call(body, outs, scratch=(), cost=(0, 0)):
    return pl.pallas_call(
        body,
        out_shape=outs,
        out_specs=jax.tree.map(lambda _: VMEM, outs),
        scratch_shapes=list(scratch),
        cost_estimate=pl.CostEstimate(flops=cost[0], bytes_accessed=cost[1], transcendentals=0),
        compiler_params=pltpu.CompilerParams(vmem_limit_bytes=24 << 20),
    )


def wrap(value, lon):
    width = value.shape[1]
    rest = lon % LANES
    first, last = value[:, :LANES], value[:, width - LANES :]
    lane = lax.broadcasted_iota(jnp.int32, last.shape, 1)
    ahead = pltpu.roll(first, rest, 1)
    behind = pltpu.roll(last, LANES - rest, 1)
    tail = jnp.where(lane < rest, last, jnp.where(lane < rest + 2, ahead, behind))
    return jnp.concatenate([value[:, : width - LANES], tail], axis=1)


def widened(value, width):
    rows, lon = value.shape
    return jnp.concatenate([value, jnp.zeros((rows, width - lon), value.dtype)], axis=1)


def cast_body(state_ref, out_ref):
    lon = state_ref.shape[-1]
    out_ref[...] = wrap(widened(state_ref[0, :, 0, :], out_ref.shape[1]), lon).astype(jnp.bfloat16)


def prepare_body(odd_ref, state_ref, seen_ref, mask_ref, noise_ref, w_ref, bias_ref, start_ref, zsq_ref, weights_ref):
    width = start_ref.shape[1]
    state, seen = state_ref[0, :, 0, :], seen_ref[0, :, 0, :]
    mask = mask_ref[0, :, 0, :].astype(jnp.float32)
    start_ref[...] = widened(state + 0.5 * (mask * (seen - state) + bias_ref[...]), width)
    noise = noise_ref[0, :, 0, :]
    zsq_ref[...] = jnp.full(zsq_ref.shape, jnp.sum(noise * noise))
    taps, window, hidden = w_ref.shape[1:]
    rows = state.shape[0]
    hours = window // rows
    for tap in range(taps):
        for slot in range(hours):
            source = jnp.where(odd_ref[0] == 1, hours - 1 - slot, slot)
            block = w_ref[0, tap, pl.ds(pl.multiple_of(source * rows, rows), rows), :]
            at = (tap * hours + slot) * rows
            weights_ref[:, at : at + rows] = block.T


def convolved(field_refs, weights_ref, bias_ref, second_ref, stack, side):
    rows, width = field_refs[0].shape
    hours = len(field_refs)
    for slot, ref in enumerate(field_refs):
        value = ref[...]
        for tap in range(3):
            at = (tap * hours + slot) * rows
            moved = value if tap == 1 else pltpu.roll(value, 1 if tap == 0 else width - 1, 1)
            stack[at : at + rows, :] = moved
    weights, second = weights_ref[...], second_ref[0].reshape(-1, second_ref.shape[-1])
    bias = bias_ref[...]
    for n in range(0, width, TILE):
        pre = jnp.dot(weights, stack[:, n : n + TILE], preferred_element_type=jnp.float32) + bias
        half = 0.5 * pre
        hidden = (half + half * jnp.tanh(half)).astype(jnp.bfloat16)
        side[:, n : n + TILE] = jnp.dot(second, hidden, preferred_element_type=jnp.float32)
    return side[rows : 2 * rows] + pltpu.roll(side[:rows], 1, 1) + pltpu.roll(side[2 * rows :], width - 1, 1)


def first_body(lon, *refs):
    fields, (weights, bias, second, start, out_ref, rounded_ref, stack, side) = refs[:5], refs[5:]
    predicted = start[...] + 0.5 * convolved(fields, weights, bias, second, stack, side)
    out_ref[...] = predicted
    rounded_ref[...] = wrap(predicted, lon).astype(jnp.bfloat16)


def second_body(lon, *refs):
    fields, rest = refs[:5], refs[5:]
    weights, bias, second, bias_two, predicted, seen_ref, mask_ref, out_ref, gsq_ref, stack, side = rest
    conv = convolved(fields, weights, bias, second, stack, side)[:, :lon]
    mask = mask_ref[0, :, 0, :].astype(jnp.float32)
    drift = conv + bias_two[...] + mask * (seen_ref[0, :, 0, :] - predicted[:, :lon])
    out_ref[...] = drift
    gsq_ref[...] = jnp.full(gsq_ref.shape, jnp.sum(drift * drift))


def last_body(sums_ref, predicted, drift, noise_ref, out_ref):
    lon = out_ref.shape[-1]
    scale = 2.0 * 0.16 * 0.16 * sums_ref[0, 0] / (sums_ref[1, 0] + 1e-06)
    step = jnp.full((1, LANES), scale)
    root = jnp.sqrt(2.0 * step)[:, :1]
    out_ref[0, :, 0, :] = predicted[:, :lon] + step[:, :1] * drift[...] + root * noise_ref[0, :, 0, :]


def exchange(field, count):
    near = [(d, d + 1) for d in range(1, count - 1, 2)] + [(d, d - 1) for d in range(2, count, 2)]
    far = [(d, d + 2) for d in range(0, count - 2, 2)] + [(d, d - 2) for d in range(3, count, 2)]
    swap = [(d, d ^ 1) for d in range(count)]
    one = lax.ppermute(field, "tm", near)
    two = lax.ppermute(field, "tm", far)
    beside = lax.ppermute(field, "tm", swap)
    passed = lax.ppermute(one, "tm", swap)
    return two, one, field, beside, passed


def summed(value, count):
    distance = 1
    while distance < count:
        value = value + lax.ppermute(value, "tm", [(d, d ^ distance) for d in range(count)])
        distance *= 2
    return value


def on_device(state, observed, obs_mask, noise, w_first, b_first, w_second, b_second):
    count = lax.axis_size("tm")
    _, rows, _, lon = state.shape
    hid = b_first.shape[0]
    width = -(-(lon + 4) // TILE) * TILE
    window = w_first.shape[1]
    f32, bf16 = jnp.float32, jnp.bfloat16
    w_one = w_first.transpose(2, 3, 1, 0)[1:2]
    w_two = w_second.transpose(2, 3, 0, 1)[1]
    bias_one, bias_two = b_first[:, None], b_second[:, None]
    odd = (lax.axis_index("tm") % 2).astype(jnp.int32).reshape(1)
    shape = jax.ShapeDtypeStruct
    field, small = shape((rows, width), bf16), shape((1, LANES), f32)

    rounded = call(cast_body, field)(state)
    start, zsq, weights = pl.pallas_call(
        prepare_body,
        in_specs=[SMEM] + [VMEM] * 6,
        out_specs=[VMEM] * 3,
        out_shape=[shape((rows, width), f32), small, shape((hid, 3 * window), bf16)],
        compiler_params=pltpu.CompilerParams(vmem_limit_bytes=24 << 20),
    )(odd, state, observed, obs_mask, noise, w_one, bias_two)
    scratch = (pltpu.VMEM((3 * window, width), bf16), pltpu.VMEM((3 * rows, width), f32))
    predicted, rounded = call(functools.partial(first_body, lon), [shape((rows, width), f32), field], scratch)(
        *exchange(rounded, count), weights, bias_one, w_two[None], start
    )
    drift, gsq = call(functools.partial(second_body, lon), [shape((rows, lon), f32), small], scratch)(
        *exchange(rounded, count), weights, bias_one, w_two[None], bias_two, predicted, observed, obs_mask
    )
    sums = summed(jnp.concatenate([zsq, gsq]), count)
    return pl.pallas_call(
        last_body,
        in_specs=[SMEM] + [VMEM] * 3,
        out_specs=VMEM,
        out_shape=shape(state.shape, f32),
        compiler_params=pltpu.CompilerParams(vmem_limit_bytes=24 << 20),
    )(sums, predicted, drift, noise)


def solution(mesh):
    return jax.shard_map(
        on_device,
        mesh=mesh,
        in_specs=(
            P(("groups", "tm"), None, None, None),
            P(("groups", "tm"), None, None, None),
            P(("groups", "tm"), None, None, None),
            P(("groups", "tm"), None, None, None),
            P(),
            P(),
            P(),
            P(),
        ),
        out_specs=P(("groups", "tm"), None, None, None),
        check_vma=False,
    )
```
